128 devices in a mesh: grp: 4 (over z_lo, core), feat: 32 (over x, y, z_hi).
Axes of the slice: x: 4, y: 4, z: 4 (z_hi: 2, z_lo: 2; z = z_hi * 2 + z_lo), core: 2. Of those that a mesh axis runs over, the one named last changes fastest.
Arguments:
- resid: bfloat16 [4, 512, 4096], P('grp', 'feat'), may hold values from -600 to 600
- norm_gain: float32 [4, 4096], P('grp'), may hold values from 0.25 to 1.75
- w_gate: bfloat16 [4, 4096, 14336], P('grp', None, 'feat'), may hold values from -0.09375 to 0.09375
- w_up: bfloat16 [4, 4096, 14336], P('grp', None, 'feat'), may hold values from -0.09375 to 0.09375
- w_down: bfloat16 [4, 14336, 4096], P('grp', 'feat'), may hold values from -0.046875 to 0.046875
- w_enc: bfloat16 [4, 4096, 16384], P('grp', None, 'feat'), may hold values from -0.09375 to 0.09375
- b_enc: float32 [4, 16384], P('grp', 'feat'), may hold values from -0.8 to 0.2
- w_dec: bfloat16 [4, 16384, 8192], P('grp', 'feat'), may hold values from -0.046875 to 0.046875
- carry_in: float32 [512, 4096], P('feat'), may hold values from -3 to 3
Outputs:
- errors: float32 [4, 512, 4096], P('grp', 'feat')
- forward: float32 [4, 512, 4096], P('grp', 'feat')
The draws below stay inside these ranges and needn't reach their ends.
All inputs are finite; a program needn't handle non-finite values.
Results may differ from the reference program's by a relative error of at most 0.0044.
Values may be sent and summed in bfloat16 or wider, within the bound.
No kernel may reach another device: no remote copies, remote signals or barrier semaphores. Data moves between devices by JAX's collectives and lax.ppermute only.
A program may use at most 128 MiB of HBM per device.

```python
import math
import jax
import jax.numpy as jnp
from jax import lax

D = 4096
FF = 14336
F = 16384
TOKENS = 512
LAYERS = 4


def draw_resid(key, part):
    key_base = jax.random.fold_in(key, 11)
    key_rows = jax.random.fold_in(key, 12)
    key_cols = jax.random.fold_in(key, 13)
    row_scale = jnp.exp(jax.random.uniform(key_rows, (LAYERS, TOKENS, 1), jnp.float32, 0.0, math.log(10.0)))
    col_scale = jnp.exp(jax.random.uniform(key_cols, (LAYERS, 1, D), jnp.float32, 0.0, math.log(10.0)))
    entries = jnp.clip(jax.random.normal(key_base, (LAYERS, TOKENS, D), jnp.float32), -5.5, 5.5)
    return (entries * row_scale * col_scale).astype(jnp.bfloat16)


def level_of(stream_key, dims, split, smallest, top_value):
    loudness, own = 1.0, jax.random.fold_in(stream_key, 6)
    for axis_at, blocks in split:
        draws = jnp.exp(jax.random.uniform(jax.random.fold_in(own, axis_at), (blocks,), jnp.float32, smallest / len(split), top_value / len(split)))
        loudness = loudness * jnp.repeat(draws, dims[axis_at] // blocks).reshape([-1 if axis == axis_at else 1 for axis in range(len(dims))])
    return loudness


def gaussian(stream_key, extent, spread, reach, shards=(), dtype=jnp.bfloat16):
    values = spread * jax.random.normal(stream_key, extent, jnp.float32)
    if shards:
        values = values * level_of(stream_key, extent, shards, -0.22, 0.18)
    return jnp.clip(values, -reach, reach).astype(dtype)


def setup_inputs(seed: int = 0) -> dict:
    keys = jax.random.split(jax.random.key(seed), 10)
    resid = draw_resid(jax.random.fold_in(keys[9], 71), 0)
    norm_gain = jnp.clip(1.0 + 0.15 * jax.random.normal(keys[1], (LAYERS, D), jnp.float32), 0.25, 1.75)
    w_gate = gaussian(keys[2], (LAYERS, D, FF), D ** -0.5, 0.09375, ((0, 4), (2, 32)))
    w_up = gaussian(keys[3], (LAYERS, D, FF), D ** -0.5, 0.09375, ((0, 4), (2, 32)))
    w_down = gaussian(keys[4], (LAYERS, FF, D), FF ** -0.5, 0.046875, ((0, 4), (1, 32)))
    w_enc = gaussian(keys[5], (LAYERS, D, F), D ** -0.5, 0.09375, ((0, 4), (2, 32)))
    b_enc = jnp.clip(-0.8 + 1 * jax.random.uniform(keys[6], (LAYERS, F), jnp.float32) ** level_of(keys[6], (LAYERS, F), ((0, 4), (1, 32)), -0.2, 0.2), -0.8, 0.2)
    w_dec = gaussian(keys[7], (LAYERS, F, 2 * D), F ** -0.5, 0.046875, ((0, 4), (1, 32)))
    carry_in = gaussian(keys[8], (TOKENS, D), 0.5, 3.0, ((0, 32),), jnp.float32)
    return dict(resid=resid, norm_gain=norm_gain, w_gate=w_gate, w_up=w_up, w_down=w_down, w_enc=w_enc, b_enc=b_enc, w_dec=w_dec, carry_in=carry_in)


def reference(resid, norm_gain, w_gate, w_up, w_down, w_enc, b_enc, w_dec, carry_in):
    error_list = []
    forward_list = []
    incoming = carry_in.astype(jnp.float32)
    for layer_idx in range(LAYERS):
        stream = resid[layer_idx].astype(jnp.float32)
        inv_rms = lax.rsqrt(lax.optimization_barrier(jnp.mean(stream * stream, axis=1, keepdims=True)) + 1e-05)
        normed = (stream * inv_rms * norm_gain[layer_idx].astype(jnp.float32)).astype(jnp.bfloat16)
        gate_sum = jnp.dot(normed, w_gate[layer_idx], preferred_element_type=jnp.float32)
        up_sum = jnp.dot(normed, w_up[layer_idx], preferred_element_type=jnp.float32)
        hidden = (jax.nn.silu(gate_sum) * up_sum).astype(jnp.bfloat16)
        mlp_out = jnp.dot(hidden, w_down[layer_idx], preferred_element_type=jnp.float32)
        pre_act = jnp.dot(normed, w_enc[layer_idx], preferred_element_type=jnp.float32) + b_enc[layer_idx].astype(jnp.float32)
        features = jax.nn.relu(pre_act).astype(jnp.bfloat16)
        decoded = jnp.dot(features, w_dec[layer_idx], preferred_element_type=jnp.float32)
        err_rows = decoded[:, :D] + incoming - mlp_out
        to_next = decoded[:, D:]
        error_list.append(err_rows)
        forward_list.append(to_next)
        incoming = to_next
    return (jnp.stack(error_list), jnp.stack(forward_list))
```

```python
import functools

import jax
import jax.numpy as jnp
from jax import lax
from jax.experimental import pallas as pl
from jax.experimental.pallas import tpu as pltpu
from jax.sharding import Mesh
from jax.sharding import PartitionSpec as P

FX, FY, FZ = "feat_0", "feat_1", "feat_2"
FEAT = (FX, FY, FZ)
BF = jnp.bfloat16
F32 = jnp.float32
VMEM = pl.BlockSpec(memory_space=pltpu.VMEM)
HBM = pl.BlockSpec(memory_space=pl.ANY)
CHEAP = pl.CostEstimate(flops=1, bytes_accessed=1, transcendentals=0)


def fetch(value, axis, ahead):
    count = lax.axis_size(axis)
    return lax.ppermute(value, axis, [((i + ahead) % count, i) for i in range(count)])


def tie(*values):
    return lax.optimization_barrier(values)


def dot(a, b):
    return jnp.dot(a, b, preferred_element_type=F32)


def dot_t(a, b):
    return lax.dot_general(a, b, (((1,), (1,)), ((), ())), preferred_element_type=F32)


def ring_gather(block, axis):
    return [block] + [fetch(block, axis, r) for r in (1, 2, 3)]


def block_orders(rows):
    own = lambda x, y: (y * 4 + x) * rows
    oth = lambda x, y: (16 + x * 4 + y) * rows
    x_first = [f(x, y) for x in range(4) for y in range(4) for f in (own, oth)]
    y_first = [f(x, y) for y in range(4) for x in range(4) for f in (own, oth)]
    return x_first, y_first


def place(act, rows, out_x, out_y):
    x_first, y_first = block_orders(rows)
    for out, order in ((out_x, x_first), (out_y, y_first)):
        for at, start in enumerate(order):
            out[at * rows:(at + 1) * rows, :] = act[start:start + rows, :]


def chunked(src, dst, sems, base, count):
    size = dst.shape[0] // count
    return [
        pltpu.make_async_copy(
            src.at[pl.ds(i * size, size), :], dst.at[pl.ds(i * size, size), :], sems.at[base + i])
        for i in range(count)
    ]


def write_parts(products, outs):
    for side in range(2):
        up, down, one, three, own = outs[side * 5:side * 5 + 5]
        far = products(2, side).astype(BF)
        mid = far.shape[0] // 2
        up[...] = far[:mid]
        down[...] = far[mid:]
        one[...] = products(1, side)
        three[...] = products(3, side)
        own[...] = products(0, side)


def part_shapes(block, half):
    far = jax.ShapeDtypeStruct((block // 2, half), BF)
    near = jax.ShapeDtypeStruct((block, half), F32)
    return [far, far, near, near, near] * 2


def fwd_kernel(rows, *refs):
    pieces, (enc, bias, dec), outs = refs[:8], refs[8:11], refs[11:21]
    feat_x, feat_y = refs[21:23]
    enc_v, dec_v, act, sems = refs[23:]
    width = enc_v.shape[0]
    copies = chunked(enc, enc_v, sems, 0, 4)
    dec_copy = pltpu.make_async_copy(dec.at[:, pl.ds(width, width)], dec_v, sems.at[4])
    for copy in copies:
        copy.start()
    dec_copy.start()
    step = width // 4
    total = None
    for i, copy in enumerate(copies):
        copy.wait()
        tokens = jnp.concatenate([p[:, i * step:(i + 1) * step] for p in pieces], axis=0)
        part = dot(tokens, enc_v[i * step:(i + 1) * step, :])
        total = part if total is None else total + part
    act[...] = jnp.maximum(total + bias[...], 0.0).astype(BF)
    place(act, rows, feat_x, feat_y)
    dec_copy.wait()
    half = width // 2
    block = 8 * rows

    def products(r, side):
        feat = (feat_x, feat_y)[side]
        return dot(feat[r * block:(r + 1) * block, :], dec_v[:, side * half:(side + 1) * half])

    write_parts(products, outs)


def err_kernel(rows, *refs):
    pieces, (feat_x, feat_y, gate, up, down, dec), outs = refs[:8], refs[8:14], refs[14:24]
    gate_v, up_v, down_v, dec_v, act, hid_x, hid_y, sems = refs[24:]
    width = gate_v.shape[1]
    hidden = gate_v.shape[0]
    copies = [
        pltpu.make_async_copy(gate, gate_v, sems.at[0]),
        pltpu.make_async_copy(up, up_v, sems.at[1]),
        pltpu.make_async_copy(down, down_v, sems.at[2]),
        pltpu.make_async_copy(dec.at[:, pl.ds(0, width)], dec_v, sems.at[3]),
    ]
    for copy in copies:
        copy.start()
    copies[0].wait()
    tokens = jnp.concatenate([p[...] for p in pieces], axis=0)
    gates = dot_t(tokens, gate_v[...])
    copies[1].wait()
    ups = dot_t(tokens, up_v[...])
    act[...] = (gates / (1.0 + jnp.exp(-gates)) * ups).astype(BF)
    place(act, rows, hid_x, hid_y)
    copies[2].wait()
    copies[3].wait()
    half = width // 2
    block = 8 * rows

    def products(r, side):
        feat, hid = ((feat_x, hid_x), (feat_y, hid_y))[side]
        at = slice(r * block, (r + 1) * block)
        cols = slice(side * half, (side + 1) * half)
        return dot(feat[at, :], dec_v[:, cols]) - dot(hid[at, :], down_v[:, cols])

    write_parts(products, outs)


def hop_far(parts, axis):
    return fetch(parts[0], axis, -1), fetch(parts[1], axis, 1)


def hop_near(parts, arrived, axis):
    up, down = (v.astype(F32) for v in arrived)
    zeros = jnp.zeros_like(up)
    ahead = parts[2] + jnp.concatenate([up, zeros], axis=0)
    behind = parts[3] + jnp.concatenate([zeros, down], axis=0)
    return fetch(ahead.astype(BF), axis, -1), fetch(behind.astype(BF), axis, 1)


def total_of(own, arrived):
    for value in arrived:
        own = own + value.astype(F32)
    return own


def split_rows(array, count):
    rows = array.shape[0] // count
    return [array[i * rows:(i + 1) * rows] for i in range(count)]


def direct(total, axis):
    parts = split_rows(total, 4)
    return parts[0], [fetch(parts[r].astype(BF), axis, -r) for r in (1, 2, 3)]


def body(resid, norm_gain, w_gate, w_up, w_down, w_enc, b_enc, w_dec, carry_in):
    rows = resid.shape[1]
    width = resid.shape[2]
    half = width // 2
    block = 8 * rows
    total_rows = 32 * rows
    stream = resid[0].astype(F32)
    inv_rms = lax.rsqrt(jnp.mean(stream * stream, axis=1, keepdims=True) + 1e-05)
    normed = (stream * inv_rms * norm_gain[0]).astype(BF)

    other = fetch(normed, FZ, 1)
    plane = jnp.concatenate(ring_gather(normed, FX), axis=0)
    other_plane = jnp.concatenate(ring_gather(other, FY), axis=0)
    plane, other_plane = tie(plane, other_plane)
    pieces = ring_gather(plane, FY) + ring_gather(other_plane, FX)

    enc, dec = w_enc[0], w_dec[0]
    features = enc.shape[1]
    shapes = part_shapes(block, half)
    order = jax.ShapeDtypeStruct((total_rows, features), BF)
    params = pltpu.CompilerParams(vmem_limit_bytes=40 << 20)
    *fwd, feat_x, feat_y = pl.pallas_call(
        functools.partial(fwd_kernel, rows),
        out_shape=shapes + [order, order],
        in_specs=[VMEM] * 8 + [HBM, VMEM, HBM],
        out_specs=[VMEM] * 12,
        scratch_shapes=[
            pltpu.VMEM(enc.shape, BF),
            pltpu.VMEM((features, width), BF),
            pltpu.VMEM((total_rows, features), BF),
            pltpu.SemaphoreType.DMA((5,)),
        ],
        compiler_params=params,
        cost_estimate=CHEAP,
        name="enc_fwd",
    )(*pieces, enc, b_enc, dec)
    fa, fb = fwd[:5], fwd[5:]

    hidden = w_gate.shape[2]
    err = pl.pallas_call(
        functools.partial(err_kernel, rows),
        out_shape=shapes,
        in_specs=[VMEM] * 10 + [HBM] * 4,
        out_specs=[VMEM] * 10,
        scratch_shapes=[
            pltpu.VMEM((hidden, width), BF),
            pltpu.VMEM((hidden, width), BF),
            pltpu.VMEM((hidden, width), BF),
            pltpu.VMEM((features, width), BF),
            pltpu.VMEM((total_rows, hidden), BF),
            pltpu.VMEM((total_rows, hidden), BF),
            pltpu.VMEM((total_rows, hidden), BF),
            pltpu.SemaphoreType.DMA((4,)),
        ],
        compiler_params=pltpu.CompilerParams(vmem_limit_bytes=48 << 20),
        cost_estimate=CHEAP,
        name="mlp_err",
    )(*pieces, feat_x, feat_y, w_gate[0].T, w_up[0].T, w_down[0], dec)
    ea, eb = err[:5], err[5:]

    f1a, f1b = hop_far(fa, FX), hop_far(fb, FY)
    e1a, e1b = hop_far(ea, FX), hop_far(eb, FY)
    f2a, f2b = hop_near(fa, f1a, FX), hop_near(fb, f1b, FY)
    e2a, e2b = hop_near(ea, e1a, FX), hop_near(eb, e1b, FY)
    sum_a = jnp.concatenate([total_of(fa[4], f2a), total_of(ea[4], e2a)], axis=1)
    sum_b = jnp.concatenate([total_of(fb[4], f2b), total_of(eb[4], e2b)], axis=1)
    da, db = direct(sum_a, FY), direct(sum_b, FX)
    low_a, low_b = total_of(*da), total_of(*db)

    def finish(cols):
        low = jnp.concatenate([low_a[:, cols], low_b[:, cols]], axis=1)
        own, oth = split_rows(low, 2)
        return own + fetch(oth.astype(BF), FZ, 1).astype(F32)

    to_next = finish(slice(0, half))
    count = lax.axis_size("grp")
    passed = lax.ppermute(to_next, "grp", [(i, i + 1) for i in range(count - 1)])
    incoming = jnp.where(lax.axis_index("grp") == 0, carry_in, passed)
    return ((finish(slice(half, width)) + incoming)[None], to_next[None])


def solution(mesh):
    finer = Mesh(
        mesh.devices.reshape(mesh.shape["grp"], 4, 4, 2), ("grp", FX, FY, FZ)
    )
    return jax.shard_map(
        body,
        mesh=finer,
        in_specs=(
            P("grp", FEAT, None),
            P("grp", None),
            P("grp", None, FEAT),
            P("grp", None, FEAT),
            P("grp", FEAT, None),
            P("grp", None, FEAT),
            P("grp", FEAT),
            P("grp", FEAT, None),
            P(FEAT, None),
        ),
        out_specs=(P("grp", FEAT, None), P("grp", FEAT, None)),
        check_vma=False,
    )
```

```python
import functools

import jax
import jax.numpy as jnp
from jax import lax
from jax.experimental import pallas as pl
from jax.experimental.pallas import tpu as pltpu
from jax.sharding import Mesh
from jax.sharding import PartitionSpec as P

FX, FY, FZ = "feat_0", "feat_1", "feat_2"
FEAT = (FX, FY, FZ)
BF = jnp.bfloat16
F32 = jnp.float32
VMEM = pl.BlockSpec(memory_space=pltpu.VMEM)
HBM = pl.BlockSpec(memory_space=pltpu.HBM)
CHEAP = pl.CostEstimate(flops=1, bytes_accessed=1, transcendentals=0)
ORDER = (2, 1, 3, 0)


def swap(value, axis, distance):
    count = lax.axis_size(axis)
    return lax.ppermute(value, axis, [(i, i ^ distance) for i in range(count)])


def tie(*values):
    return lax.optimization_barrier(values)


def dot(a, b):
    return jnp.dot(a, b, preferred_element_type=F32)


def dot_t(a, b):
    return lax.dot_general(a, b, (((1,), (1,)), ((), ())), preferred_element_type=F32)


def ring_gather(block, axis):
    return [block, swap(block, axis, 1), swap(block, axis, 3)]


def ring_relay(pieces, axis):
    _, one, three = pieces
    half = one.shape[0] // 2
    return [swap(one[:half], axis, 3), swap(three[half:], axis, 1)]


def block_orders(rows):
    slot = {0: 0, 1: 1, 3: 2}
    own = lambda x, y: ((slot[y] if y != 2 else 6) * 4 + x) * rows
    oth = lambda x, y: ((3 + slot[x] if x != 2 else 7) * 4 + y) * rows
    x_first = [f(x, y) for x in ORDER for y in range(4) for f in (own, oth)]
    y_first = [f(x, y) for y in ORDER for x in range(4) for f in (own, oth)]
    return x_first, y_first


def place(first, rest, rows, out_x, out_y):
    early = first.shape[0]
    x_first, y_first = block_orders(rows)
    for out, order in ((out_x, x_first), (out_y, y_first)):
        for at, start in enumerate(order):
            src, start = (first, start) if start < early else (rest, start - early)
            out[at * rows:(at + 1) * rows, :] = src[start:start + rows, :]


def feature_units(tokens, enc, bias):
    return jnp.maximum(dot(tokens, enc[...]) + bias[...], 0.0).astype(BF)


def hidden_units(tokens, gate, up):
    gates = dot_t(tokens, gate[...])
    ups = dot_t(tokens, up[...])
    return (gates / (1.0 + jnp.exp(-gates)) * ups).astype(BF)


def load_kernel(_, *refs):
    count = (len(refs) - 1) // 2
    copies = [pltpu.make_async_copy(refs[i], refs[count + i], refs[-1].at[i]) for i in range(count)]
    for copy in copies:
        copy.start()
    for copy in copies:
        copy.wait()


def first_kernel(*refs):
    pieces, (enc, bias, gate, up), (feat, hid) = refs[:6], refs[6:10], refs[10:]
    tokens = jnp.concatenate([p[...] for p in pieces], axis=0)
    feat[...] = feature_units(tokens, enc, bias)
    hid[...] = hidden_units(tokens, gate, up)


def products(feat, hid, down, dec, at, side):
    width = down.shape[1]
    half = width // 2
    f, h = feat[at, :], hid[at, :]
    cols = slice(side * half, (side + 1) * half)
    ahead = slice(width + side * half, width + (side + 1) * half)
    yield slice(0, half), dot(f, dec[:, ahead])
    yield slice(half, width), dot(f, dec[:, cols]) - dot(h, down[:, cols])


def far_kernel(rows, *refs):
    pieces, (feat, hid, enc, bias, gate, up, down, dec), outs = refs[:4], refs[4:12], refs[12:16]
    feat_x, feat_y, hid_x, hid_y, feat_late, hid_late = refs[16:]
    tokens = jnp.concatenate([p[...] for p in pieces], axis=0)
    feat_late[...] = feature_units(tokens, enc, bias)
    hid_late[...] = hidden_units(tokens, gate, up)
    place(feat, feat_late, rows, feat_x, feat_y)
    place(hid, hid_late, rows, hid_x, hid_y)
    mid = 4 * rows
    for side, (f, h) in enumerate(((feat_x, hid_x), (feat_y, hid_y))):
        for cols, value in products(f, h, down, dec, slice(0, 2 * mid), side):
            outs[2 * side][:, cols] = value[:mid].astype(BF)
            outs[2 * side + 1][:, cols] = value[mid:].astype(BF)


def near_kernel(rows, feat_x, feat_y, hid_x, hid_y, down, dec, *outs):
    block = 8 * rows
    for side, (f, h) in enumerate(((feat_x, hid_x), (feat_y, hid_y))):
        for cols, value in products(f, h, down, dec, slice(block, 4 * block), side):
            for at in range(3):
                outs[3 * side + at][:, cols] = value[at * block:(at + 1) * block]


def hop_far(parts, axis):
    return swap(parts[0], axis, 1), swap(parts[1], axis, 3)


def hop_near(parts, arrived, axis):
    upper, lower = (v.astype(F32) for v in arrived)
    zeros = jnp.zeros_like(upper)
    one = parts[0] + jnp.concatenate([zeros, lower], axis=0)
    three = parts[1] + jnp.concatenate([upper, zeros], axis=0)
    return swap(one.astype(BF), axis, 1), swap(three.astype(BF), axis, 3)


def total_of(own, arrived):
    for value in arrived:
        own = own + value.astype(F32)
    return own


def split_rows(array, count):
    rows = array.shape[0] // count
    return [array[i * rows:(i + 1) * rows] for i in range(count)]


def direct(total, axis):
    parts = split_rows(total, 4)
    return parts[0], [swap(parts[r].astype(BF), axis, r) for r in (1, 2, 3)]


def body(resid, norm_gain, w_gate, w_up, w_down, w_enc, b_enc, w_dec, carry_in):
    rows = resid.shape[1]
    width = resid.shape[2]
    half = width // 2
    block = 8 * rows
    stream = resid[0].astype(F32)
    inv_rms = lax.rsqrt(jnp.mean(stream * stream, axis=1, keepdims=True) + 1e-05)
    normed = (stream * inv_rms * norm_gain[0]).astype(BF)

    other = swap(normed, FZ, 1)
    plane = jnp.concatenate([normed] + [swap(normed, FX, r) for r in (1, 2, 3)], axis=0)
    other_plane = jnp.concatenate([other] + [swap(other, FY, r) for r in (1, 2, 3)], axis=0)
    plane, other_plane = tie(plane, other_plane)
    own_early = ring_gather(plane, FY)
    oth_early = ring_gather(other_plane, FX)

    enc, dec, down, gate, up = w_enc[0], w_dec[0], w_down[0], w_gate[0].T, w_up[0].T
    features, hidden = enc.shape[1], down.shape[0]

    def shape(count, cols, dtype=BF):
        return jax.ShapeDtypeStruct((count, cols), dtype)

    def call(kernel, name, ins, outs, scratch, limit):
        return pl.pallas_call(
            kernel,
            out_shape=outs,
            in_specs=ins,
            out_specs=[VMEM] * len(outs),
            scratch_shapes=scratch,
            compiler_params=pltpu.CompilerParams(vmem_limit_bytes=limit << 20),
            cost_estimate=CHEAP,
            name=name,
        )

    weights = (enc, gate, up, down, dec)
    enc, gate, up, down, dec = call(
        load_kernel, "load_weights", [VMEM] + [HBM] * 5, [shape(*w.shape) for w in weights],
        [pltpu.SemaphoreType.DMA((5,))], 4,
    )(plane, *weights)
    *late, enc, gate, up, down, dec = tie(*own_early, *oth_early, enc, gate, up, down, dec)
    own_early, oth_early = late[:3], late[3:]
    own_late, oth_late = ring_relay(own_early, FY), ring_relay(oth_early, FX)
    early = 24 * rows
    feat, hid = call(
        first_kernel, "first_units", [VMEM] * 10, [shape(early, features), shape(early, hidden)], [], 12,
    )(*own_early, *oth_early, enc, b_enc, gate, up)
    *far_parts, feat_x, feat_y, hid_x, hid_y = call(
        functools.partial(far_kernel, rows), "far_parts", [VMEM] * 12,
        [shape(block // 2, width)] * 4 + [shape(4 * block, features)] * 2 + [shape(4 * block, hidden)] * 2,
        [pltpu.VMEM((block, features), BF), pltpu.VMEM((block, hidden), BF)], 12,
    )(*own_late, *oth_late, feat, hid, enc, b_enc, gate, up, down, dec)
    far_a, far_b = hop_far(far_parts[:2], FX), hop_far(far_parts[2:], FY)
    near_parts = call(
        functools.partial(near_kernel, rows), "near_parts", [VMEM] * 6,
        [shape(block, width, F32)] * 6, [], 12,
    )(feat_x, feat_y, hid_x, hid_y, down, dec)
    near_a = hop_near(near_parts[:2], far_a, FX)
    near_b = hop_near(near_parts[3:5], far_b, FY)
    da = direct(total_of(near_parts[2], near_a), FY)
    db = direct(total_of(near_parts[5], near_b), FX)
    low_a, low_b = total_of(*da), total_of(*db)

    def halves(cols):
        return split_rows(jnp.concatenate([low_a[:, cols], low_b[:, cols]], axis=1), 2)

    fwd_own, fwd_oth = halves(slice(0, half))
    err_own, err_oth = halves(slice(half, width))
    fwd_oth = fwd_oth.astype(BF)
    count = lax.axis_size("grp")
    onward = [(i, i + 1) for i in range(count - 1)]
    planes = lax.axis_size(FZ)
    crossed = [(i * planes + z, (i + 1) * planes + (z ^ 1)) for i in range(count - 1) for z in range(planes)]
    arrived, passed, passed_oth = tie(
        swap(jnp.concatenate([fwd_oth, err_oth.astype(BF)], axis=1), FZ, 1),
        lax.ppermute(fwd_own, "grp", onward),
        lax.ppermute(fwd_oth, ("grp", FZ), crossed),
    )
    arrived = arrived.astype(F32)
    incoming = jnp.where(lax.axis_index("grp") == 0, carry_in, passed + passed_oth.astype(F32))
    to_next = fwd_own + arrived[:, :width]
    errors = err_own + arrived[:, width:] + incoming
    return (errors[None], to_next[None])


def solution(mesh):
    finer = Mesh(
        mesh.devices.reshape(mesh.shape["grp"], 4, 4, 2), ("grp", FX, FY, FZ)
    )
    return jax.shard_map(
        body,
        mesh=finer,
        in_specs=(
            P("grp", FEAT, None),
            P("grp", None),
            P("grp", None, FEAT),
            P("grp", None, FEAT),
            P("grp", FEAT, None),
            P("grp", None, FEAT),
            P("grp", FEAT),
            P("grp", FEAT, None),
            P(FEAT, None),
        ),
        out_specs=(P("grp", FEAT, None), P("grp", FEAT, None)),
        check_vma=False,
    )
```

```python
import functools

import jax
import jax.numpy as jnp
from jax import lax
from jax.experimental import pallas as pl
from jax.experimental.pallas import tpu as pltpu
from jax.sharding import Mesh
from jax.sharding import PartitionSpec as P

FX, FY, FZ = "feat_0", "feat_1", "feat_2"
FEAT = (FX, FY, FZ)
BF = jnp.bfloat16
F32 = jnp.float32
VMEM = pl.BlockSpec(memory_space=pltpu.VMEM)
HBM = pl.BlockSpec(memory_space=pltpu.HBM)
CHEAP = pl.CostEstimate(flops=1, bytes_accessed=1, transcendentals=0)
ORDER = (2, 1, 3, 0)


def swap(value, axis, distance):
    count = lax.axis_size(axis)
    return lax.ppermute(value, axis, [(i, i ^ distance) for i in range(count)])


def tie(*values):
    return lax.optimization_barrier(values)


def dot(a, b):
    return jnp.dot(a, b, preferred_element_type=F32)


def dot_t(a, b):
    return lax.dot_general(a, b, (((1,), (1,)), ((), ())), preferred_element_type=F32)


def ring_gather(block, axis):
    return [block, swap(block, axis, 1), swap(block, axis, 3)]


def ring_relay(pieces, axis):
    _, one, three = pieces
    half = one.shape[0] // 2
    return [swap(one[:half], axis, 3), swap(three[half:], axis, 1)]


def block_orders(rows):
    slot = {0: 0, 1: 1, 3: 2}
    own = lambda x, y: ((slot[y] if y != 2 else 6) * 4 + x) * rows
    oth = lambda x, y: ((3 + slot[x] if x != 2 else 7) * 4 + y) * rows
    x_first = [f(x, y) for x in ORDER for y in range(4) for f in (own, oth)]
    y_first = [f(x, y) for y in ORDER for x in range(4) for f in (own, oth)]
    return x_first, y_first


def place(first, rest, rows, out_x, out_y):
    early = first.shape[0]
    x_first, y_first = block_orders(rows)
    for out, order in ((out_x, x_first), (out_y, y_first)):
        for at, start in enumerate(order):
            src, start = (first, start) if start < early else (rest, start - early)
            out[at * rows:(at + 1) * rows, :] = src[start:start + rows, :]


def feature_units(tokens, enc, bias):
    return jnp.maximum(dot(tokens, enc[...]) + bias[...], 0.0).astype(BF)


def hidden_units(tokens, gate, up):
    gates = dot_t(tokens, gate[...])
    ups = dot_t(tokens, up[...])
    return (gates / (1.0 + jnp.exp(-gates)) * ups).astype(BF)


def norm_kernel(resid, gain, out):
    stream = resid[...].astype(F32)
    inv_rms = lax.rsqrt(jnp.mean(stream * stream, axis=1, keepdims=True) + 1e-05)
    out[...] = (stream * inv_rms * gain[...]).astype(BF)


def load_kernel(_, *refs):
    count = (len(refs) - 1) // 2
    copies = [pltpu.make_async_copy(refs[i], refs[count + i], refs[-1].at[i]) for i in range(count)]
    for copy in copies:
        copy.start()
    for copy in copies:
        copy.wait()


def first_kernel(*refs):
    pieces, (enc, bias, gate, up), (feat, hid) = refs[:6], refs[6:10], refs[10:]
    tokens = jnp.concatenate([p[...] for p in pieces], axis=0)
    feat[...] = feature_units(tokens, enc, bias)
    hid[...] = hidden_units(tokens, gate, up)


def products(feat, hid, down, dec, at, side):
    width = down.shape[1]
    half = width // 2
    f, h = feat[at, :], hid[at, :]
    cols = slice(side * half, (side + 1) * half)
    ahead = slice(width + side * half, width + (side + 1) * half)
    yield slice(0, half), dot(f, dec[:, ahead])
    yield slice(half, width), dot(f, dec[:, cols]) - dot(h, down[:, cols])


def far_kernel(rows, *refs):
    pieces, (feat, hid, enc, bias, gate, up, down, dec), outs = refs[:4], refs[4:12], refs[12:16]
    feat_x, feat_y, hid_x, hid_y, feat_late, hid_late = refs[16:]
    tokens = jnp.concatenate([p[...] for p in pieces], axis=0)
    feat_late[...] = feature_units(tokens, enc, bias)
    hid_late[...] = hidden_units(tokens, gate, up)
    place(feat, feat_late, rows, feat_x, feat_y)
    place(hid, hid_late, rows, hid_x, hid_y)
    mid = 4 * rows
    for side, (f, h) in enumerate(((feat_x, hid_x), (feat_y, hid_y))):
        for cols, value in products(f, h, down, dec, slice(0, 2 * mid), side):
            outs[2 * side][:, cols] = value[:mid].astype(BF)
            outs[2 * side + 1][:, cols] = value[mid:].astype(BF)


def near_kernel(rows, feat_x, feat_y, hid_x, hid_y, down, dec, *outs):
    block = 8 * rows
    for side, (f, h) in enumerate(((feat_x, hid_x), (feat_y, hid_y))):
        for cols, value in products(f, h, down, dec, slice(block, 4 * block), side):
            for at in range(3):
                outs[3 * side + at][:, cols] = value[at * block:(at + 1) * block]


def hop_far(parts, axis):
    return swap(parts[0], axis, 1), swap(parts[1], axis, 3)


def hop_near(parts, arrived, axis):
    upper, lower = (v.astype(F32) for v in arrived)
    zeros = jnp.zeros_like(upper)
    one = parts[0] + jnp.concatenate([zeros, lower], axis=0)
    three = parts[1] + jnp.concatenate([upper, zeros], axis=0)
    return swap(one.astype(BF), axis, 1), swap(three.astype(BF), axis, 3)


def total_of(own, arrived):
    for value in arrived:
        own = own + value.astype(F32)
    return own


def split_rows(array, count):
    rows = array.shape[0] // count
    return [array[i * rows:(i + 1) * rows] for i in range(count)]


def direct(total, axis):
    parts = split_rows(total, 4)
    return parts[0], [swap(parts[r].astype(BF), axis, r) for r in (1, 2, 3)]


def body(resid, norm_gain, w_gate, w_up, w_down, w_enc, b_enc, w_dec, carry_in):
    rows = resid.shape[1]
    width = resid.shape[2]
    half = width // 2
    block = 8 * rows
    def shape(count, cols, dtype=BF):
        return jax.ShapeDtypeStruct((count, cols), dtype)

    def call(kernel, name, ins, outs, scratch, limit):
        return pl.pallas_call(
            kernel,
            out_shape=outs,
            in_specs=ins,
            out_specs=[VMEM] * len(outs),
            scratch_shapes=scratch,
            compiler_params=pltpu.CompilerParams(vmem_limit_bytes=limit << 20),
            cost_estimate=CHEAP,
            name=name,
        )

    def norm(stream):
        return call(norm_kernel, "norm", [VMEM] * 2, [shape(rows, width)], [], 4)(stream, norm_gain)[0]

    other = swap(resid[0], FZ, 1)
    normed = norm(resid[0])
    other = norm(other)
    plane = jnp.concatenate([normed] + [swap(normed, FX, r) for r in (1, 2, 3)], axis=0)
    other_plane = jnp.concatenate([other] + [swap(other, FY, r) for r in (1, 2, 3)], axis=0)
    plane = tie(plane, other)[0]
    own_early = ring_gather(plane, FY)
    oth_early = ring_gather(other_plane, FX)

    enc, dec, down, gate, up = w_enc[0], w_dec[0], w_down[0], w_gate[0].T, w_up[0].T
    features, hidden = enc.shape[1], down.shape[0]

    weights = (enc, gate, up)
    enc, gate, up = call(
        load_kernel, "load_weights", [VMEM] + [HBM] * 3, [shape(*w.shape) for w in weights],
        [pltpu.SemaphoreType.DMA((3,))], 4,
    )(plane, *weights)
    *own_early, enc, gate, up = tie(*own_early, enc, gate, up)
    *oth_early, enc, gate, up = tie(*oth_early, enc, gate, up)
    own_late, oth_late = ring_relay(own_early, FY), ring_relay(oth_early, FX)
    early = 24 * rows
    feat, hid = call(
        first_kernel, "first_units", [VMEM] * 10, [shape(early, features), shape(early, hidden)], [], 12,
    )(*own_early, *oth_early, enc, b_enc, gate, up)
    *far_parts, feat_x, feat_y, hid_x, hid_y = call(
        functools.partial(far_kernel, rows), "far_parts", [VMEM] * 12,
        [shape(block // 2, width)] * 4 + [shape(4 * block, features)] * 2 + [shape(4 * block, hidden)] * 2,
        [pltpu.VMEM((block, features), BF), pltpu.VMEM((block, hidden), BF)], 12,
    )(*own_late, *oth_late, feat, hid, enc, b_enc, gate, up, down, dec)
    far_a, far_b = hop_far(far_parts[:2], FX), hop_far(far_parts[2:], FY)
    near_parts = call(
        functools.partial(near_kernel, rows), "near_parts", [VMEM] * 6,
        [shape(block, width, F32)] * 6, [], 12,
    )(feat_x, feat_y, hid_x, hid_y, down, dec)
    near_a = hop_near(near_parts[:2], far_a, FX)
    near_b = hop_near(near_parts[3:5], far_b, FY)
    da = direct(total_of(near_parts[2], near_a), FY)
    db = direct(total_of(near_parts[5], near_b), FX)
    low_a, low_b = total_of(*da), total_of(*db)

    def halves(cols):
        return split_rows(jnp.concatenate([low_a[:, cols], low_b[:, cols]], axis=1), 2)

    fwd_own, fwd_oth = halves(slice(0, half))
    err_own, err_oth = halves(slice(half, width))
    fwd_oth = fwd_oth.astype(BF)
    count = lax.axis_size("grp")
    onward = [(i, i + 1) for i in range(count - 1)]
    planes = lax.axis_size(FZ)
    crossed = [(i * planes + z, (i + 1) * planes + (z ^ 1)) for i in range(count - 1) for z in range(planes)]
    arrived, passed, passed_oth = tie(
        swap(jnp.concatenate([fwd_oth, err_oth.astype(BF)], axis=1), FZ, 1),
        lax.ppermute(fwd_own, "grp", onward),
        lax.ppermute(fwd_oth, ("grp", FZ), crossed),
    )
    arrived = arrived.astype(F32)
    incoming = jnp.where(lax.axis_index("grp") == 0, carry_in, passed + passed_oth.astype(F32))
    to_next = fwd_own + arrived[:, :width]
    errors = err_own + arrived[:, width:] + incoming
    return (errors[None], to_next[None])


def solution(mesh):
    finer = Mesh(
        mesh.devices.reshape(mesh.shape["grp"], 4, 4, 2), ("grp", FX, FY, FZ)
    )
    return jax.shard_map(
        body,
        mesh=finer,
        in_specs=(
            P("grp", FEAT, None),
            P("grp", None),
            P("grp", None, FEAT),
            P("grp", None, FEAT),
            P("grp", FEAT, None),
            P("grp", None, FEAT),
            P("grp", FEAT),
            P("grp", FEAT, None),
            P(FEAT, None),
        ),
        out_specs=(P("grp", FEAT, None), P("grp", FEAT, None)),
        check_vma=False,
    )
```

```python
import functools

import jax
import jax.numpy as jnp
from jax import lax
from jax.experimental import pallas as pl
from jax.experimental.pallas import tpu as pltpu
from jax.sharding import Mesh
from jax.sharding import PartitionSpec as P

FX, FY, FZ = "feat_0", "feat_1", "feat_2"
FEAT = (FX, FY, FZ)
BF = jnp.bfloat16
F32 = jnp.float32
VMEM = pl.BlockSpec(memory_space=pltpu.VMEM)
HBM = pl.BlockSpec(memory_space=pltpu.HBM)
CHEAP = pl.CostEstimate(flops=1, bytes_accessed=1, transcendentals=0)
ORDER = (2, 1, 3, 0)


def swap(value, axis, distance):
    count = lax.axis_size(axis)
    return lax.ppermute(value, axis, [(i, i ^ distance) for i in range(count)])


def tie(*values):
    return lax.optimization_barrier(values)


def dot(a, b):
    return jnp.dot(a, b, preferred_element_type=F32)


def dot_t(a, b):
    return lax.dot_general(a, b, (((1,), (1,)), ((), ())), preferred_element_type=F32)


def ring_gather(block, axis):
    return [block, swap(block, axis, 1), swap(block, axis, 3)]


def ring_relay(pieces, axis):
    _, one, three = pieces
    half = one.shape[0] // 2
    return [swap(one[:half], axis, 3), swap(three[half:], axis, 1)]


def block_orders(rows):
    slot = {0: 0, 1: 1, 3: 2}
    own = lambda x, y: ((slot[y] if y != 2 else 6) * 4 + x) * rows
    oth = lambda x, y: ((3 + slot[x] if x != 2 else 7) * 4 + y) * rows
    x_first = [f(x, y) for x in ORDER for y in range(4) for f in (own, oth)]
    y_first = [f(x, y) for y in ORDER for x in range(4) for f in (own, oth)]
    return x_first, y_first


def place(first, rest, out, order, rows):
    early = first.shape[0]
    for at, start in enumerate(order):
        src, start = (first, start) if start < early else (rest, start - early)
        out[at * rows:(at + 1) * rows, :] = src[start:start + rows, :]


def feature_units(tokens, enc, bias):
    return jnp.maximum(dot(tokens, enc[...]) + bias[...], 0.0).astype(BF)


def hidden_units(tokens, gate, up):
    gates = dot_t(tokens, gate[...])
    ups = dot_t(tokens, up[...])
    return (gates / (1.0 + jnp.exp(-gates)) * ups).astype(BF)


def norm_kernel(resid, gain, out):
    stream = resid[...].astype(F32)
    inv_rms = lax.rsqrt(jnp.mean(stream * stream, axis=1, keepdims=True) + 1e-05)
    out[...] = (stream * inv_rms * gain[...]).astype(BF)


def load_kernel(_, *refs):
    count = (len(refs) - 1) // 2
    copies = [pltpu.make_async_copy(refs[i], refs[count + i], refs[-1].at[i]) for i in range(count)]
    for copy in copies:
        copy.start()
    for copy in copies:
        copy.wait()


def first_kernel(*refs):
    pieces, (enc, bias, gate, up), (feat, hid) = refs[:6], refs[6:10], refs[10:]
    tokens = jnp.concatenate([p[...] for p in pieces], axis=0)
    feat[...] = feature_units(tokens, enc, bias)
    hid[...] = hidden_units(tokens, gate, up)


def forward_part(feat, dec, at):
    width = dec.shape[1] // 2
    return dot(feat[at, :], dec[:, width:])


def error_part(feat, hid, down, dec, at):
    width = dec.shape[1] // 2
    return dot(feat[at, :], dec[:, :width]) - dot(hid[at, :], down[...])


def far_kernel(rows, *refs):
    pieces, (feat, hid, enc, bias, gate, up, down, dec), outs = refs[:4], refs[4:12], refs[12:16]
    feat_x, feat_y, hid_y, feat_late, hid_late = refs[16:]
    tokens = jnp.concatenate([p[...] for p in pieces], axis=0)
    x_first, y_first = block_orders(rows)
    feat_late[...] = feature_units(tokens, enc, bias)
    hid_late[...] = hidden_units(tokens, gate, up)
    place(feat, feat_late, feat_x, x_first, rows)
    place(feat, feat_late, feat_y, y_first, rows)
    place(hid, hid_late, hid_y, y_first, rows)
    mid = 4 * rows
    far = slice(0, 2 * mid)
    for side, value in enumerate((forward_part(feat_x, dec, far), error_part(feat_y, hid_y, down, dec, far))):
        outs[2 * side][...] = value[:mid].astype(BF)
        outs[2 * side + 1][...] = value[mid:].astype(BF)


def near_kernel(rows, feat_x, feat_y, hid_y, down, dec, *outs):
    block = 8 * rows
    near = slice(block, 4 * block)
    for side, value in enumerate((forward_part(feat_x, dec, near), error_part(feat_y, hid_y, down, dec, near))):
        for at in range(3):
            outs[3 * side + at][...] = value[at * block:(at + 1) * block]


def hop_far(parts, axis):
    return swap(parts[0], axis, 1), swap(parts[1], axis, 3)


def near_rows(parts, arrived):
    upper, lower = (v.astype(F32) for v in arrived)
    zeros = jnp.zeros_like(upper)
    one = parts[0] + jnp.concatenate([zeros, lower], axis=0)
    three = parts[1] + jnp.concatenate([upper, zeros], axis=0)
    return one.astype(BF), three.astype(BF)


def after(values, others):
    return tie(*values, *others)[:len(values)]


def hop_near(rows, axis):
    return swap(rows[0], axis, 1), swap(rows[1], axis, 3)


def sum_kernel(own, near, behind, rest, *sends):
    total = own[...] + near[...].astype(F32) + behind[...].astype(F32)
    count = rest.shape[0]
    rest[...] = total[:count]
    for at, out in enumerate(sends, 1):
        out[...] = total[at * count:(at + 1) * count].astype(BF)


def last_kernel(rest, one, two, three, own, other):
    total = rest[...] + one[...].astype(F32) + two[...].astype(F32) + three[...].astype(F32)
    count = own.shape[0]
    own[...] = total[:count]
    other[...] = total[count:].astype(BF)


def body(resid, norm_gain, w_gate, w_up, w_down, w_enc, b_enc, w_dec, carry_in):
    rows = resid.shape[1]
    width = resid.shape[2]
    block = 8 * rows
    def shape(count, cols, dtype=BF):
        return jax.ShapeDtypeStruct((count, cols), dtype)

    def call(kernel, name, ins, outs, scratch, limit):
        return pl.pallas_call(
            kernel,
            out_shape=outs,
            in_specs=ins,
            out_specs=[VMEM] * len(outs),
            scratch_shapes=scratch,
            compiler_params=pltpu.CompilerParams(vmem_limit_bytes=limit << 20),
            cost_estimate=CHEAP,
            name=name,
        )

    def norm(stream):
        return call(norm_kernel, "norm", [VMEM] * 2, [shape(rows, width)], [], 4)(stream, norm_gain)[0]

    other = swap(resid[0], FZ, 1)
    normed = norm(resid[0])
    other = norm(other)
    plane = jnp.concatenate([normed] + [swap(normed, FX, r) for r in (1, 2, 3)], axis=0)
    other_plane = jnp.concatenate([other] + [swap(other, FY, r) for r in (1, 2, 3)], axis=0)
    plane = tie(plane, other)[0]
    own_early = ring_gather(plane, FY)
    oth_early = ring_gather(other_plane, FX)

    enc, dec, down, gate, up = w_enc[0], w_dec[0], w_down[0], w_gate[0].T, w_up[0].T
    features, hidden = enc.shape[1], down.shape[0]

    weights = (enc, gate, up)
    enc, gate, up = call(
        load_kernel, "load_weights", [VMEM] + [HBM] * 3, [shape(*w.shape) for w in weights],
        [pltpu.SemaphoreType.DMA((3,))], 4,
    )(plane, *weights)
    *own_early, enc, gate, up = tie(*own_early, enc, gate, up)
    *oth_early, enc, gate, up = tie(*oth_early, enc, gate, up)
    own_late, oth_late = ring_relay(own_early, FY), ring_relay(oth_early, FX)
    early = 24 * rows
    feat, hid = call(
        first_kernel, "first_units", [VMEM] * 10, [shape(early, features), shape(early, hidden)], [], 12,
    )(*own_early, *oth_early, enc, b_enc, gate, up)
    *far_parts, feat_x, feat_y, hid_y = call(
        functools.partial(far_kernel, rows), "far_parts", [VMEM] * 12,
        [shape(block // 2, width)] * 4 + [shape(4 * block, features)] * 2 + [shape(4 * block, hidden)],
        [pltpu.VMEM((block, features), BF), pltpu.VMEM((block, hidden), BF)], 12,
    )(*own_late, *oth_late, feat, hid, enc, b_enc, gate, up, down, dec)
    far_f, far_e = hop_far(far_parts[:2], FX), hop_far(far_parts[2:], FY)
    near_parts = call(
        functools.partial(near_kernel, rows), "near_parts", [VMEM] * 5,
        [shape(block, width, F32)] * 6, [], 12,
    )(feat_x, feat_y, hid_y, down, dec)
    rows_f = near_rows(near_parts[:2], far_f)
    near_f = hop_near(rows_f, FX)
    near_e = hop_near(near_rows(near_parts[3:5], after(far_e, rows_f)), FY)
    quarter = 2 * rows

    def second_stage(own, arrived, axis):
        rest, *sends = call(
            sum_kernel, "first_sums", [VMEM] * 3,
            [shape(quarter, width, F32)] + [shape(quarter, width)] * 3, [], 8,
        )(own, *arrived)
        return rest, sends, [swap(part, axis, r) for r, part in enumerate(sends, 1)]

    def last_sums(rest, arrived):
        return call(
            last_kernel, "second_sums", [VMEM] * 4, [shape(rows, width, F32), shape(rows, width)], [], 4,
        )(rest, *arrived)

    rest_f, sends_f, arrived_f = second_stage(near_parts[2], near_f, FY)
    rest_e, sends_e, arrived_e = second_stage(near_parts[5], after(near_e, sends_f), FX)
    arrived_f = after(arrived_f, sends_e)
    fwd_own, fwd_oth = last_sums(rest_f, arrived_f)
    count, planes = lax.axis_size("grp"), lax.axis_size(FZ)
    onward = [(i, i + 1) for i in range(count - 1)]
    crossed = [(i * planes + z, (i + 1) * planes + (z ^ 1)) for i in range(count - 1) for z in range(planes)]
    passed_oth = lax.ppermute(fwd_oth, ("grp", FZ), crossed)
    arrived = swap(fwd_oth, FZ, 1)
    passed = lax.ppermute(fwd_own, "grp", onward)
    err_own, err_oth = last_sums(rest_e, arrived_e)
    err_arrived = swap(err_oth, FZ, 1)
    incoming = jnp.where(lax.axis_index("grp") == 0, carry_in, passed + passed_oth.astype(F32))
    to_next = fwd_own + arrived.astype(F32)
    errors = err_own + err_arrived.astype(F32) + incoming
    return (errors[None], to_next[None])


def solution(mesh):
    finer = Mesh(
        mesh.devices.reshape(mesh.shape["grp"], 4, 4, 2), ("grp", FX, FY, FZ)
    )
    return jax.shard_map(
        body,
        mesh=finer,
        in_specs=(
            P("grp", FEAT, None),
            P("grp", None),
            P("grp", None, FEAT),
            P("grp", None, FEAT),
            P("grp", FEAT, None),
            P("grp", None, FEAT),
            P("grp", FEAT),
            P("grp", FEAT, None),
            P(FEAT, None),
        ),
        out_specs=(P("grp", FEAT, None), P("grp", FEAT, None)),
        check_vma=False,
    )
```

```python
import functools

import jax
import jax.numpy as jnp
from jax import lax
from jax.experimental import pallas as pl
from jax.experimental.pallas import tpu as pltpu
from jax.sharding import Mesh
from jax.sharding import PartitionSpec as P

FX, FY, FZ = "feat_0", "feat_1", "feat_2"
FEAT = (FX, FY, FZ)
BF = jnp.bfloat16
F32 = jnp.float32
VMEM = pl.BlockSpec(memory_space=pltpu.VMEM)
HBM = pl.BlockSpec(memory_space=pltpu.HBM)
CHEAP = pl.CostEstimate(flops=1, bytes_accessed=1, transcendentals=0)
ORDER = (2, 1, 3, 0)


def swap(value, axis, distance):
    count = lax.axis_size(axis)
    return lax.ppermute(value, axis, [(i, i ^ distance) for i in range(count)])


def tie(*values):
    return lax.optimization_barrier(values)


def dot(a, b):
    return jnp.dot(a, b, preferred_element_type=F32)


def dot_t(a, b):
    return lax.dot_general(a, b, (((1,), (1,)), ((), ())), preferred_element_type=F32)


def row_of(block, axis):
    two, one, three = (swap(block, axis, r) for r in (2, 1, 3))
    return jnp.concatenate([block, one, two, three], axis=0)


def ring_gather(block, axis):
    return [block, swap(block, axis, 1), swap(block, axis, 3)]


def ring_relay(pieces, axis):
    _, one, three = pieces
    half = one.shape[0] // 2
    return [swap(one[:half], axis, 3), swap(three[half:], axis, 1)]


def block_orders(rows):
    slot = {0: 0, 1: 1, 3: 2}
    own = lambda x, y: ((slot[y] if y != 2 else 6) * 4 + x) * rows
    oth = lambda x, y: ((3 + slot[x] if x != 2 else 7) * 4 + y) * rows
    x_first = [f(x, y) for x in ORDER for y in range(4) for f in (own, oth)]
    y_first = [f(x, y) for y in ORDER for x in range(4) for f in (own, oth)]
    return x_first, y_first


def place(first, rest, out, order, rows):
    early = first.shape[0]
    for at, start in enumerate(order):
        src, start = (first, start) if start < early else (rest, start - early)
        out[at * rows:(at + 1) * rows, :] = src[start:start + rows, :]


def feature_units(tokens, enc, bias):
    return jnp.maximum(dot(tokens, enc[...]) + bias[...], 0.0).astype(BF)


def hidden_units(tokens, gate, up):
    gates = dot_t(tokens, gate[...])
    ups = dot_t(tokens, up[...])
    return (gates / (1.0 + jnp.exp(-gates)) * ups).astype(BF)


def norm_kernel(resid, gain, out):
    stream = resid[...].astype(F32)
    inv_rms = lax.rsqrt(jnp.mean(stream * stream, axis=1, keepdims=True) + 1e-05)
    out[...] = (stream * inv_rms * gain[...]).astype(BF)


def load_kernel(_, *refs):
    count = (len(refs) - 1) // 2
    copies = [pltpu.make_async_copy(refs[i], refs[count + i], refs[-1].at[i]) for i in range(count)]
    for copy in copies:
        copy.start()
    for copy in copies:
        copy.wait()


def first_kernel(*refs):
    pieces, (enc, bias, gate, up), (feat, hid) = refs[:6], refs[6:10], refs[10:]
    tokens = jnp.concatenate([p[...] for p in pieces], axis=0)
    feat[...] = feature_units(tokens, enc, bias)
    hid[...] = hidden_units(tokens, gate, up)


def forward_part(feat, dec, at):
    width = dec.shape[1] // 2
    return dot(feat[at, :], dec[:, width:])


def error_part(feat, hid, down, dec, at):
    width = dec.shape[1] // 2
    return dot(feat[at, :], dec[:, :width]) - dot(hid[at, :], down[...])


def far_kernel(rows, *refs):
    pieces, (feat, hid, enc, bias, gate, up, down, dec), outs = refs[:4], refs[4:12], refs[12:16]
    feat_x, feat_y, hid_y, feat_late, hid_late = refs[16:]
    tokens = jnp.concatenate([p[...] for p in pieces], axis=0)
    x_first, y_first = block_orders(rows)
    feat_late[...] = feature_units(tokens, enc, bias)
    hid_late[...] = hidden_units(tokens, gate, up)
    place(feat, feat_late, feat_x, x_first, rows)
    place(feat, feat_late, feat_y, y_first, rows)
    place(hid, hid_late, hid_y, y_first, rows)
    mid = 4 * rows
    far = slice(0, 2 * mid)
    for side, value in enumerate((forward_part(feat_x, dec, far), error_part(feat_y, hid_y, down, dec, far))):
        outs[2 * side][...] = value[:mid].astype(BF)
        outs[2 * side + 1][...] = value[mid:].astype(BF)


def near_kernel(rows, feat_x, feat_y, hid_y, down, dec, *outs):
    block = 8 * rows
    near = slice(block, 4 * block)
    for side, value in enumerate((forward_part(feat_x, dec, near), error_part(feat_y, hid_y, down, dec, near))):
        for at in range(3):
            outs[3 * side + at][...] = value[at * block:(at + 1) * block]


def hop_far(parts, axis):
    return swap(parts[0], axis, 1), swap(parts[1], axis, 3)


def near_rows(parts, arrived):
    upper, lower = (v.astype(F32) for v in arrived)
    zeros = jnp.zeros_like(upper)
    one = parts[0] + jnp.concatenate([zeros, lower], axis=0)
    three = parts[1] + jnp.concatenate([upper, zeros], axis=0)
    return one.astype(BF), three.astype(BF)


def after(values, others):
    return tie(*values, *others)[:len(values)]


def hop_near(rows, axis):
    return swap(rows[0], axis, 1), swap(rows[1], axis, 3)


def sum_kernel(own, near, behind, rest, *sends):
    total = own[...] + near[...].astype(F32) + behind[...].astype(F32)
    count = rest.shape[0]
    rest[...] = total[:count]
    for at, out in enumerate(sends, 1):
        out[...] = total[at * count:(at + 1) * count].astype(BF)


def last_kernel(rest, one, two, three, own, other):
    total = rest[...] + one[...].astype(F32) + two[...].astype(F32) + three[...].astype(F32)
    count = own.shape[0]
    own[...] = total[:count]
    other[...] = total[count:].astype(BF)


def body(resid, norm_gain, w_gate, w_up, w_down, w_enc, b_enc, w_dec, carry_in):
    rows = resid.shape[1]
    width = resid.shape[2]
    block = 8 * rows
    def shape(count, cols, dtype=BF):
        return jax.ShapeDtypeStruct((count, cols), dtype)

    def call(kernel, name, ins, outs, scratch, limit):
        return pl.pallas_call(
            kernel,
            out_shape=outs,
            in_specs=ins,
            out_specs=[VMEM] * len(outs),
            scratch_shapes=scratch,
            compiler_params=pltpu.CompilerParams(vmem_limit_bytes=limit << 20),
            cost_estimate=CHEAP,
            name=name,
        )

    def norm(stream):
        return call(norm_kernel, "norm", [VMEM] * 2, [shape(rows, width)], [], 4)(stream, norm_gain)[0]

    other = swap(resid[0], FZ, 1)
    normed = norm(resid[0])
    other = norm(other)
    plane = row_of(normed, FX)
    other_plane = row_of(other, FY)
    plane = tie(plane, other)[0]
    own_early = ring_gather(plane, FY)
    oth_early = ring_gather(other_plane, FX)

    enc, dec, down, gate, up = w_enc[0], w_dec[0], w_down[0], w_gate[0].T, w_up[0].T
    features, hidden = enc.shape[1], down.shape[0]

    weights = (enc, gate, up)
    enc, gate, up = call(
        load_kernel, "load_weights", [VMEM] + [HBM] * 3, [shape(*w.shape) for w in weights],
        [pltpu.SemaphoreType.DMA((3,))], 4,
    )(plane, *weights)
    *own_early, enc, gate, up = tie(*own_early, enc, gate, up)
    *oth_early, enc, gate, up = tie(*oth_early, enc, gate, up)
    own_late, oth_late = ring_relay(own_early, FY), ring_relay(oth_early, FX)
    early = 24 * rows
    feat, hid = call(
        first_kernel, "first_units", [VMEM] * 10, [shape(early, features), shape(early, hidden)], [], 12,
    )(*own_early, *oth_early, enc, b_enc, gate, up)
    *far_parts, feat_x, feat_y, hid_y = call(
        functools.partial(far_kernel, rows), "far_parts", [VMEM] * 12,
        [shape(block // 2, width)] * 4 + [shape(4 * block, features)] * 2 + [shape(4 * block, hidden)],
        [pltpu.VMEM((block, features), BF), pltpu.VMEM((block, hidden), BF)], 12,
    )(*own_late, *oth_late, feat, hid, enc, b_enc, gate, up, down, dec)
    far_f, far_e = hop_far(far_parts[:2], FX), hop_far(far_parts[2:], FY)
    near_parts = call(
        functools.partial(near_kernel, rows), "near_parts", [VMEM] * 5,
        [shape(block, width, F32)] * 6, [], 12,
    )(feat_x, feat_y, hid_y, down, dec)
    rows_f = near_rows(near_parts[:2], far_f)
    near_f = hop_near(rows_f, FX)
    near_e = hop_near(near_rows(near_parts[3:5], after(far_e, rows_f)), FY)
    quarter = 2 * rows

    def second_stage(own, arrived, axis):
        rest, *sends = call(
            sum_kernel, "first_sums", [VMEM] * 3,
            [shape(quarter, width, F32)] + [shape(quarter, width)] * 3, [], 8,
        )(own, *arrived)
        return rest, sends, [swap(sends[r - 1], axis, r) for r in (2, 1, 3)]

    def last_sums(rest, arrived):
        return call(
            last_kernel, "second_sums", [VMEM] * 4, [shape(rows, width, F32), shape(rows, width)], [], 4,
        )(rest, *arrived)

    rest_f, sends_f, arrived_f = second_stage(near_parts[2], near_f, FY)
    rest_e, sends_e, arrived_e = second_stage(near_parts[5], after(near_e, sends_f), FX)
    arrived_f = after(arrived_f, sends_e)
    fwd_own, fwd_oth = last_sums(rest_f, arrived_f)
    count, planes = lax.axis_size("grp"), lax.axis_size(FZ)
    onward = [(i, i + 1) for i in range(count - 1)]
    crossed = [(i * planes + z, (i + 1) * planes + (z ^ 1)) for i in range(count - 1) for z in range(planes)]
    passed_oth = lax.ppermute(fwd_oth, ("grp", FZ), crossed)
    arrived = swap(fwd_oth, FZ, 1)
    passed = lax.ppermute(fwd_own, "grp", onward)
    err_own, err_oth = last_sums(rest_e, arrived_e)
    err_arrived = swap(err_oth, FZ, 1)
    incoming = jnp.where(lax.axis_index("grp") == 0, carry_in, passed + passed_oth.astype(F32))
    to_next = fwd_own + arrived.astype(F32)
    errors = err_own + err_arrived.astype(F32) + incoming
    return (errors[None], to_next[None])


def solution(mesh):
    finer = Mesh(
        mesh.devices.reshape(mesh.shape["grp"], 4, 4, 2), ("grp", FX, FY, FZ)
    )
    return jax.shard_map(
        body,
        mesh=finer,
        in_specs=(
            P("grp", FEAT, None),
            P("grp", None),
            P("grp", None, FEAT),
            P("grp", None, FEAT),
            P("grp", FEAT, None),
            P("grp", None, FEAT),
            P("grp", FEAT),
            P("grp", FEAT, None),
            P(FEAT, None),
        ),
        out_specs=(P("grp", FEAT, None), P("grp", FEAT, None)),
        check_vma=False,
    )
```
